32 devices in a mesh: pole: 2 (over core), row: 4 (over y, x), col: 4 (over z).
Axes of the slice: x: 2, y: 2, z: 4, core: 2. Of those that a mesh axis runs over, the one named last changes fastest.
Arguments:
- inverse_trail: bfloat16 [2, 1024, 2, 1024], P('pole', 'row', None, 'col'), may hold values from -6 to 6
- lower_t: bfloat16 [2, 2048, 2, 1024], P('pole', 'col', None, 'row'), may hold values from -0.125 to 0.125
- diag_inverse: bfloat16 [2, 2048, 2, 2048], P('pole', 'row', None, 'col'), may hold values from -6 to 6
- pole_weight: float32 [256, 2], replicated, may hold values from -4 to 4
- pole_slot: int32 [2], P('pole'), may hold values from 0 to 255
- pair_row: int32 [1024], replicated, may hold values from 0 to 383, as said below
- pair_col: int32 [1024], replicated, may hold values from 0 to 255, as said below
- projector: bfloat16 [1024, 64], P('pole'), may hold values from -6 to 6
Outputs:
- diag_block: bfloat16 [2, 2048, 2, 2048], P('pole', 'row', None, 'col')
- pair_density: float32 [1024, 128], P('pole')
The draws below stay inside these ranges and needn't reach their ends.
Inputs may be any that keep to these rules, and one draw needn't show every extreme that they name: `pair_row`: pairs come in aligned blocks of 512, one block for each index of pole. A pair's grid cell is (a // (256 // size of row), b // (256 // size of col)) for a supernode row atom a and column atom b, and (b // (256 // size of row), (a - 256) // (128 // size of col)) otherwise. In every block at most 64 pairs share one grid cell, and some cell holds exactly 64. `pair_col`: drawn together with pair_row.
All inputs are finite; a program needn't handle non-finite values.
Results may differ from the reference program's by a relative error of at most 0.0038.
Values may be sent and summed in bfloat16 or wider, within the bound.
A program may use at most 64 MiB of HBM per device.

```python
import jax
import jax.numpy as jnp
from jax import lax

K = 2048
M = 1024
B = 8
WTAB = 256
PAIR_DEV = 512
POLES = 2
KA = 256
MA = 128
NPAIR = 1024
N_POLE = 2
N_ROW = 4
N_COL = 4


def pair_layout(key):
    base = jax.random.fold_in(key, 7711)
    cells = N_ROW * N_COL
    most = 2 * PAIR_DEV // cells
    keys = jax.random.split(base, 7)
    first = jax.random.randint(keys[0], (N_POLE,), 0, cells)
    block_keys = jax.random.split(keys[1], N_POLE)
    others = jax.vmap(lambda k: jax.random.permutation(k, cells - 1))(block_keys)
    place = jnp.arange(PAIR_DEV, dtype=jnp.int32)
    spread = jnp.take_along_axis(others, jnp.broadcast_to(jnp.maximum(place - most, 0) % (cells - 1), (N_POLE, PAIR_DEV)), axis=1)
    spread = (first[:, None] + 1 + spread) % cells
    cell = jnp.where(place[None, :] < most, first[:, None], spread)
    order_keys = jax.random.split(keys[2], N_POLE)
    orders = jax.vmap(lambda k: jax.random.permutation(k, PAIR_DEV))(order_keys)
    cell = jnp.take_along_axis(cell, orders, axis=1).reshape(NPAIR)
    grid_row = cell // N_COL
    grid_col = cell % N_COL
    row_atoms = KA // N_ROW
    col_atoms = KA // N_COL
    trail_atoms = MA // N_COL
    is_super = jax.random.randint(keys[3], (NPAIR,), 0, 2) == 1
    first_pick = jax.random.randint(keys[4], (NPAIR,), 0, 1 << 20)
    second_pick = jax.random.randint(keys[5], (NPAIR,), 0, 1 << 20)
    other_pick = jax.random.randint(keys[6], (NPAIR,), 0, 1 << 20)
    low_pick = jnp.minimum(first_pick, second_pick)
    super_row = grid_row * row_atoms + low_pick % row_atoms
    super_col = grid_col * col_atoms + other_pick % col_atoms
    trail_row = KA + grid_col * trail_atoms + low_pick % trail_atoms
    trail_col = grid_row * row_atoms + other_pick % row_atoms
    rows = jnp.where(is_super, super_row, trail_row).astype(jnp.int32)
    columns = jnp.where(is_super, super_col, trail_col).astype(jnp.int32)
    return (rows, columns)


def draw_pair_row(key, part):
    return pair_layout(key)[0]


def draw_pair_col(key, part):
    return pair_layout(key)[1]


def level_of(key, dims, cuts, low, top_value):
    factor_of = 1.0
    for dim, blocks in cuts:
        steps = jax.random.uniform(jax.random.fold_in(jax.random.fold_in(key, 6), dim), (blocks,), jnp.float32, low / len(cuts), top_value / len(cuts))
        factor_of = factor_of * jnp.repeat(jnp.exp(steps), dims[dim] // blocks).reshape((-1,) + (1,) * (len(dims) - 1 - dim))
    return factor_of


def bell_draw(key, dims, width, most, cuts=(), kind=jnp.bfloat16):
    drawn = jax.random.normal(key, dims, jnp.float32) * width
    if len(cuts) > 0:
        drawn = level_of(key, dims, cuts, -0.22, 0.18) * drawn
    return jnp.clip(drawn, min=-most, max=most).astype(kind)


def setup_inputs(seed: int = 0) -> dict:
    streams_of = jax.random.split(jax.random.key(seed), 9)
    inverse_trail = bell_draw(streams_of[0], (POLES, M, 2, M), 1.0, 6.0, ((0, 2), (1, 4), (3, 4)))
    lower_t = bell_draw(streams_of[1], (POLES, K, 2, M), (2 * M) ** -0.5, 0.125, ((0, 2), (1, 4), (3, 4)))
    diag_inverse = bell_draw(streams_of[2], (POLES, K, 2, K), 1.0, 6.0, ((0, 2), (1, 4), (3, 4)))
    pole_weight = bell_draw(streams_of[3], (WTAB, 2), 1.0, 4.0, (), jnp.float32)
    pole_slot = jax.random.randint(streams_of[4], (POLES,), 0, WTAB).astype(jnp.int32)
    pair_row = draw_pair_row(jax.random.fold_in(streams_of[8], 71), 0)
    pair_col = draw_pair_col(jax.random.fold_in(streams_of[8], 71), 0)
    projector = bell_draw(streams_of[7], (NPAIR, B * B), 1.0, 6.0, ((0, 2),))
    return dict(inverse_trail=inverse_trail, lower_t=lower_t, diag_inverse=diag_inverse, pole_weight=pole_weight, pole_slot=pole_slot, pair_row=pair_row, pair_col=pair_col, projector=projector)


def cproduct(left_side, right_side):
    real_a = left_side[:, 0, :]
    imag_a = left_side[:, 1, :]
    real_b = right_side[:, 0, :]
    imag_b = right_side[:, 1, :]
    real_out = jnp.dot(real_a, real_b, preferred_element_type=jnp.float32) - jnp.dot(imag_a, imag_b, preferred_element_type=jnp.float32)
    imag_out = jnp.dot(real_a, imag_b, preferred_element_type=jnp.float32) + jnp.dot(imag_a, real_b, preferred_element_type=jnp.float32)
    return jnp.stack([real_out, imag_out], axis=1)


def reference(inverse_trail, lower_t, diag_inverse, pole_weight, pole_slot, pair_row, pair_col, projector):
    weights = pole_weight[pole_slot]
    in_super = pair_row < KA
    super_index = jnp.minimum(pair_row, KA - 1)
    trail_index = jnp.clip(pair_row - KA, 0, MA - 1)

    def one_pole(packed):
        trail, lower, inverse, weight = packed
        coupling = (-cproduct(lower, trail)).astype(jnp.bfloat16)
        lower_swap = jnp.transpose(lower, (2, 1, 0))
        block = (inverse.astype(jnp.float32) - cproduct(coupling, lower_swap)).astype(jnp.bfloat16)
        table_super = block.reshape(KA, B, 2, KA, B).transpose(0, 3, 2, 1, 4)
        table_trail = coupling.reshape(KA, B, 2, MA, B).transpose(3, 0, 2, 4, 1)
        from_super = table_super[super_index, pair_col]
        from_trail = table_trail[trail_index, pair_col]
        chosen = jnp.where(in_super[:, None, None, None], from_super, from_trail)
        chosen = chosen.astype(jnp.float32).reshape(NPAIR, 2, B * B)
        real_part = weight[0] * chosen[:, 0] - weight[1] * chosen[:, 1]
        imag_part = weight[0] * chosen[:, 1] + weight[1] * chosen[:, 0]
        return block, jnp.stack([real_part, imag_part], axis=1)

    blocks, weighted = lax.map(one_pole, (inverse_trail, lower_t, diag_inverse, weights))
    summed = jnp.sum(weighted, axis=0)
    density = summed * projector.astype(jnp.float32)[:, None, :]
    return blocks, density.reshape(NPAIR, 2 * B * B)
```

```python
import functools

import jax
import jax.numpy as jnp
from jax import lax
from jax.experimental import pallas as pl
from jax.experimental.pallas import tpu as pltpu
from jax.sharding import PartitionSpec as P

B = 8
HALVES = 2
MESH = pl.DeviceIdType.MESH


def main_kernel(
    n, l_ref, t_ref, inv_ref, idx_ref, weight_ref, proj_ref, block_ref, dens_ref,
    term, pool, coll, slots, term_send, term_recv, coll_send, coll_recv, prod_ref,
    lz, lx, part, own, rs, cz, treal,
    lz_send, lz_recv, lx_send, lx_recv, rs_send, rs_recv, cz_send, cz_recv,
):
    r = lax.axis_index("row")
    c = lax.axis_index("col")
    size = l_ref.shape[0]
    half = size // HALVES
    step = min(128, half)
    width = t_ref.shape[0]
    bf16 = jnp.bfloat16
    f32 = jnp.float32

    barrier = pltpu.get_barrier_semaphore()
    me = lax.axis_index("pole")
    owners = lax.axis_size("pole")
    cells = n * n
    cell = r * n + c

    def peer(j):
        other = lax.rem(cell + j, cells)
        return {"row": other // n, "col": lax.rem(other, n)}, other

    for j in range(1, cells):
        pl.semaphore_signal(barrier, inc=1, device_id=peer(j)[0], device_id_type=MESH)
    for j in range(1, owners):
        pl.semaphore_signal(barrier, inc=1, device_id={"pole": lax.rem(me + j, owners)}, device_id_type=MESH)
    pl.semaphore_wait(barrier, cells - 1 + owners - 1)

    def rows(h):
        return pl.ds(h * half, half)

    def line_copy(src, dst, send, recv, k, h, side):
        to = jnp.maximum(c - 1, 0) if side == 0 else jnp.minimum(c + 1, n - 1)
        return pltpu.make_async_remote_copy(
            src_ref=src,
            dst_ref=dst.at[k, rows(h)],
            send_sem=send.at[side, k, h],
            recv_sem=recv.at[k, h],
            device_id={"col": to},
            device_id_type=MESH,
        )

    def can(side):
        return c > 0 if side == 0 else c < n - 1

    def from_side(side, s):
        k = c + s if side == 0 else c - s
        there = k < n if side == 0 else k >= 0
        return jnp.clip(k, 0, n - 1), there

    def l_copy(k, h, side, mine):
        src = l_ref.at[rows(h)] if mine else lz.at[k, rows(h)]
        return line_copy(src, lz, lz_send, lz_recv, k, h, side)

    def c_copy(k, h, side):
        return line_copy(cz.at[k, rows(h)], cz, cz_send, cz_recv, k, h, side)

    def lx_copy(j):
        return pltpu.make_async_remote_copy(
            src_ref=l_ref,
            dst_ref=lx.at[r],
            send_sem=lx_send.at[j],
            recv_sem=lx_recv.at[r],
            device_id={"row": lax.rem(r + j, n)},
            device_id_type=MESH,
        )

    def lx_wait(j):
        k = lax.rem(r + j, n)
        pltpu.make_async_remote_copy(
            src_ref=l_ref, dst_ref=lx.at[k], send_sem=lx_send.at[j], recv_sem=lx_recv.at[k],
            device_id={"row": k}, device_id_type=MESH,
        ).wait_recv()

    def rs_copy(k, h):
        return pltpu.make_async_remote_copy(
            src_ref=part.at[k, rows(h)],
            dst_ref=rs.at[r, rows(h)],
            send_sem=rs_send.at[k, h],
            recv_sem=rs_recv.at[r, h],
            device_id={"row": k},
            device_id_type=MESH,
        )

    def rs_wait(j, h):
        k = lax.rem(r + j, n)
        pltpu.make_async_remote_copy(
            src_ref=part.at[k, rows(h)], dst_ref=rs.at[k, rows(h)], send_sem=rs_send.at[k, h],
            recv_sem=rs_recv.at[k, h], device_id={"row": k}, device_id_type=MESH,
        ).wait_recv()

    def partial(k, h, mine):
        def one(i, carry):
            at = pl.ds(pl.multiple_of(h * half + i * step, step), step)
            left = l_ref[at] if mine else lz[k, at]
            value = -jnp.dot(left, treal[...], preferred_element_type=f32)

            @pl.when(k == r)
            def _():
                own[at] = value

            @pl.when(k != r)
            def _():
                part[k, at] = value.astype(bf16)

            return carry

        lax.fori_loop(0, half // step, one, 0)

        @pl.when(k != r)
        def _():
            rs_copy(k, h).start()

    def finish():
        for h in range(HALVES):
            for j in range(1, n):
                rs_wait(j, h)

            def one(i, carry):
                at = pl.ds(pl.multiple_of(h * half + i * step, step), step)
                total = own[at]
                for j in range(1, n):
                    total = total + rs[lax.rem(r + j, n), at].astype(f32)
                value = total.astype(bf16)
                cz[c, at] = value
                return carry

            lax.fori_loop(0, half // step, one, 0)
            for side in range(2):
                @pl.when(can(side))
                def _():
                    c_copy(c, h, side).start()

    def accumulate(k, first):
        def with_right(right):
            real = right[:, :width]
            imag = right[:, width:]
            right_re = jnp.concatenate([real, -imag], axis=1)
            right_im = jnp.concatenate([imag, real], axis=1)

            def one(i, carry):
                at = pl.ds(pl.multiple_of(i * step, step), step)
                left = cz[k, at]
                dims = (((1,), (1,)), ((), ()))
                re = lax.dot_general(left, right_re, dims, preferred_element_type=f32)
                im = lax.dot_general(left, right_im, dims, preferred_element_type=f32)
                if first:
                    prod_ref[at, :size] = re
                    prod_ref[at, size:] = im
                else:
                    prod_ref[at, :size] += re
                    prod_ref[at, size:] += im
                return carry

            lax.fori_loop(0, size // step, one, 0)

        @pl.when(k == r)
        def _():
            with_right(l_ref[...])

        @pl.when(k != r)
        def _():
            with_right(lx[k])

    for h in range(HALVES):
        for side in range(2):
            @pl.when(can(side))
            def _():
                l_copy(c, h, side, True).start()

    trail_re = t_ref[:, :width]
    trail_im = t_ref[:, width:]
    treal[:width, :width] = trail_re
    treal[:width, width:] = trail_im
    treal[width:, :width] = -trail_im
    treal[width:, width:] = trail_re
    for h in range(HALVES):
        partial(c, h, True)
    lx_copy(1).start()

    per_owner = idx_ref.shape[2]
    most = 2 * per_owner // cells
    held_rows = most * B
    chunk = min(128, held_rows)
    earlier = (
        lax.broadcasted_iota(jnp.int32, (per_owner, per_owner), 0)
        < lax.broadcasted_iota(jnp.int32, (per_owner, per_owner), 1)
    ).astype(f32).astype(bf16)

    def ranks(o):
        cell_of = idx_ref[o, 0:1, :]
        marks = cell_of == lax.broadcasted_iota(jnp.int32, (cells, per_owner), 0).astype(f32)
        marks = jnp.where(marks, 1.0, 0.0)
        before = jnp.dot(marks.astype(bf16), earlier, preferred_element_type=f32)
        return cell_of, jnp.sum(marks * before, axis=0, keepdims=True)

    def index_owner(o, carry):
        cell_of, rank = ranks(o)
        place = jnp.where(cell_of == cell.astype(f32), rank, -1.0)

        def index_chunk(i, inner):
            slot = (lax.broadcasted_iota(jnp.int32, (chunk, per_owner), 0) + i * chunk) >> 3
            pick = jnp.where(place == slot.astype(f32), 1.0, 0.0)
            at = pl.ds(pl.multiple_of(i * chunk, chunk), chunk)
            for v in range(3):
                value = jnp.sum(pick * idx_ref[o, v + 1 : v + 2, :], axis=1, keepdims=True)
                slots[o, v, at] = jnp.broadcast_to(value, (chunk, 128))
            return inner

        lax.fori_loop(0, held_rows // chunk, index_chunk, 0)
        return carry

    lax.fori_loop(0, owners, index_owner, 0)
    apart = jnp.abs(r - c)
    for s in range(1, n):
        for h in range(HALVES):
            for side in range(2):
                k, there = from_side(side, s)

                @pl.when(there)
                def _():
                    l_copy(k, h, side, False).wait_recv()

                    @pl.when(can(side))
                    def _():
                        l_copy(k, h, side, False).start()

            for side in range(2):
                k, there = from_side(side, s)

                @pl.when(there)
                def _():
                    partial(k, h, False)

        if s + 1 < n:
            lx_copy(s + 1).start()
        if s >= 2:
            @pl.when(apart == s - 2)
            def _():
                finish()

    @pl.when(apart >= n - 2)
    def _():
        finish()

    for j in range(1, n):
        lx_wait(j)
    for t in range(1, n):
        for h in range(HALVES):
            for side in range(2):
                k, there = from_side(side, t)

                @pl.when(there)
                def _():
                    c_copy(k, h, side).wait_recv()

                    @pl.when(can(side))
                    def _():
                        c_copy(k, h, side).start()

        if t == 1:
            accumulate(c, True)
        else:
            for side in range(2):
                k, there = from_side(side, t - 1)

                @pl.when(there)
                def _():
                    accumulate(k, False)

    for side in range(2):
        k, there = from_side(side, n - 1)

        @pl.when(there)
        def _():
            accumulate(k, False)

    def write(i, carry):
        at = pl.ds(pl.multiple_of(i * step, step), step)
        block_ref[at] = (inv_ref[at].astype(f32) - prod_ref[at]).astype(bf16)
        return carry

    lax.fori_loop(0, size // step, write, 0)

    lanes = 2 * B * B
    part_lanes = B * B

    def spread(total, transposed):
        at = lax.broadcasted_iota(jnp.int32, (2 * total, lanes), 0)
        to = lax.broadcasted_iota(jnp.int32, (2 * total, lanes), 1)
        half_of = (at >= total) == (to >= part_lanes)
        inner = ((to & (part_lanes - 1)) >> 3) if transposed else (to & 7)
        return jnp.where(half_of & ((at & 7) == inner), 1.0, 0.0).astype(bf16)

    spread_super = spread(size, False)
    spread_trail = spread(width, True)
    lane = lax.broadcasted_iota(jnp.int32, (chunk, lanes), 1)
    inside = lax.broadcasted_iota(jnp.int32, (chunk, lanes), 0) & 7
    keep_super = ((lane & (part_lanes - 1)) >> 3) == inside
    keep_trail = (lane & 7) == inside
    group = jnp.where(
        lax.broadcasted_iota(jnp.int32, (chunk // B, chunk), 0)
        == (lax.broadcasted_iota(jnp.int32, (chunk // B, chunk), 1) >> 3),
        1.0,
        0.0,
    ).astype(bf16)
    row_of = lax.broadcasted_iota(jnp.int32, (chunk, size), 1).astype(f32)
    row_in = (lax.broadcasted_iota(jnp.int32, (chunk, 1), 0) & 7).astype(f32)
    col_super = lax.broadcasted_iota(jnp.int32, (chunk, 2 * size), 1)
    col_super = jnp.where(col_super >= size, col_super - size, col_super).astype(f32)
    col_trail = lax.broadcasted_iota(jnp.int32, (chunk, 2 * width), 1)
    col_trail = jnp.where(col_trail >= width, col_trail - width, col_trail).astype(f32)
    last = float(B - 1)

    def gather_owner(o, carry):
        def gather_chunk(i, inner):
            at = pl.ds(pl.multiple_of(i * chunk, chunk), chunk)
            first_row = slots[o, 0, at][:, :1]
            first_super = slots[o, 1, at][:, :1]
            first_trail = slots[o, 2, at][:, :1]
            pick = jnp.where(row_of == first_row + row_in, 1.0, 0.0).astype(bf16)
            taken = jnp.dot(pick, block_ref[...], preferred_element_type=f32)
            taken = jnp.where(
                (col_super >= first_super) & (col_super <= first_super + last), taken, 0.0
            ).astype(bf16)
            out_super = jnp.dot(taken, spread_super, preferred_element_type=f32)
            taken = jnp.dot(pick, cz[c], preferred_element_type=f32)
            taken = jnp.where(
                (col_trail >= first_trail) & (col_trail <= first_trail + last), taken, 0.0
            ).astype(bf16)
            out_trail = jnp.dot(taken, spread_trail, preferred_element_type=f32)
            both = jnp.where(keep_super, out_super, 0.0) + jnp.where(keep_trail, out_trail, 0.0)
            value = jnp.dot(group, both.astype(bf16), preferred_element_type=f32)
            swapped = jnp.concatenate([value[:, part_lanes:], value[:, :part_lanes]], axis=1)
            to = pl.ds(pl.multiple_of(i * (chunk // B), chunk // B), chunk // B)
            term[o, to] = weight_ref[0:1] * value + weight_ref[1:2] * swapped
            return inner

        lax.fori_loop(0, held_rows // chunk, gather_chunk, 0)
        return carry

    lax.fori_loop(0, owners, gather_owner, 0)

    def term_copy(j):
        to = lax.rem(me + j, owners)
        return pltpu.make_async_remote_copy(
            src_ref=term.at[to], dst_ref=pool.at[j], send_sem=term_send.at[j],
            recv_sem=term_recv.at[j], device_id={"pole": to}, device_id_type=MESH,
        )

    for j in range(1, owners):
        term_copy(j).start()
    for j in range(1, owners):
        term_copy(j).wait_recv()
    total = term[me]
    for j in range(1, owners):
        total = total + pool[j]
    coll[cell] = total

    def coll_copy(j):
        return pltpu.make_async_remote_copy(
            src_ref=coll.at[cell], dst_ref=coll.at[cell], send_sem=coll_send.at[j],
            recv_sem=coll_recv.at[cell], device_id=peer(j)[0], device_id_type=MESH,
        )

    def coll_wait(j):
        where, other = peer(j)
        pltpu.make_async_remote_copy(
            src_ref=coll.at[other], dst_ref=coll.at[other], send_sem=coll_send.at[j],
            recv_sem=coll_recv.at[other], device_id=where, device_id_type=MESH,
        ).wait_recv()

    for j in range(1, cells):
        coll_copy(j).start()
    cell_of, rank = ranks(me)
    target = jnp.broadcast_to(cell_of * most + rank, (128, per_owner))
    target = jnp.transpose(target)
    for j in range(1, cells):
        coll_wait(j)
    for q in range(per_owner // 128):
        mine = target[q * 128 : (q + 1) * 128, :1]
        pick = jnp.where(
            mine == lax.broadcasted_iota(jnp.int32, (128, cells * most), 1).astype(f32), 1.0, 0.0
        ).astype(bf16)
        rest = coll[...].reshape(cells * most, lanes)
        summed = jnp.zeros((128, lanes), f32)
        for _ in range(3):
            top = rest.astype(bf16)
            rest = rest - top.astype(f32)
            summed = summed + jnp.dot(pick, top, preferred_element_type=f32)
        dens_ref[q * 128 : (q + 1) * 128] = summed * proj_ref[q * 128 : (q + 1) * 128]

    for j in range(1, owners):
        term_copy(j).wait_send()
    for j in range(1, cells):
        coll_copy(j).wait_send()
    for j in range(1, n):
        lx_copy(j).wait_send()
        for h in range(HALVES):
            rs_copy(lax.rem(r + j, n), h).wait_send()
    for s in range(n):
        for h in range(HALVES):
            for side in range(2):
                k, there = from_side(side, s)

                @pl.when(there & can(side))
                def _():
                    l_copy(k, h, side, s == 0).wait_send()
                    c_copy(k, h, side).wait_send()


def products(n, owners, lower, trail, inverse, idx, weight, projector):
    size = lower.shape[0]
    wide = lower.shape[1]
    bf16 = jnp.bfloat16
    lanes = 2 * B * B
    most = 2 * idx.shape[2] // (n * n)
    dma = pltpu.SemaphoreType.DMA
    vmem = pl.BlockSpec(memory_space=pltpu.VMEM)
    return pl.pallas_call(
        functools.partial(main_kernel, n),
        name="products",
        out_shape=(
            jax.ShapeDtypeStruct((size, 2 * size), bf16),
            jax.ShapeDtypeStruct(projector.shape, jnp.float32),
        ),
        in_specs=[vmem] * 6,
        out_specs=(vmem, vmem),
        scratch_shapes=[
            pltpu.VMEM((owners, most, lanes), jnp.float32),
            pltpu.VMEM((owners, most, lanes), jnp.float32),
            pltpu.VMEM((n * n, most, lanes), jnp.float32),
            pltpu.VMEM((owners, 3, most * B, 128), jnp.float32),
            dma((owners,)),
            dma((owners,)),
            dma((n * n,)),
            dma((n * n,)),
            pltpu.VMEM((size, 2 * size), jnp.float32),
            pltpu.VMEM((n, size, wide), bf16),
            pltpu.VMEM((n, size, wide), bf16),
            pltpu.VMEM((n, size, wide), bf16),
            pltpu.VMEM((size, wide), jnp.float32),
            pltpu.VMEM((n, size, wide), bf16),
            pltpu.VMEM((n, size, wide), bf16),
            pltpu.VMEM((wide, wide), bf16),
            dma((2, n, HALVES)),
            dma((n, HALVES)),
            dma((n,)),
            dma((n,)),
            dma((n, HALVES)),
            dma((n, HALVES)),
            dma((2, n, HALVES)),
            dma((n, HALVES)),
        ],
        compiler_params=pltpu.CompilerParams(
            collective_id=0, has_side_effects=True, vmem_limit_bytes=40 * 1024 * 1024
        ),
    )(lower, trail, inverse, idx, weight, projector)


def local(
    inverse_trail, lower_t, diag_inverse, pole_weight, pole_slot, pair_row, pair_col, projector
):
    trail = inverse_trail[0]
    lower = lower_t[0]
    inverse = diag_inverse[0]
    n = lax.axis_size("row")
    owners = lax.axis_size("pole")
    f32 = jnp.float32
    size = lower.shape[0]
    atoms = size // B
    trail_atoms = trail.shape[2] // B
    in_super = pair_row < atoms * n
    trail_atom = jnp.maximum(pair_row - atoms * n, 0)
    row_atom = jnp.where(in_super, pair_row, pair_col)
    col_atom = jnp.where(in_super, pair_col, trail_atom)
    cell_row = row_atom // atoms
    cell_col = jnp.where(in_super, col_atom // atoms, col_atom // trail_atoms)
    away = -8 * size
    row_first = (row_atom - cell_row * atoms) * B
    super_first = jnp.where(in_super, (col_atom - cell_col * atoms) * B, away)
    trail_first = jnp.where(in_super, away, (col_atom - cell_col * trail_atoms) * B)
    idx = jnp.stack(
        [
            x.reshape(owners, -1).astype(f32)
            for x in (cell_row * n + cell_col, row_first, super_first, trail_first)
        ],
        axis=1,
    )
    selector = (jnp.arange(pole_weight.shape[0], dtype=jnp.int32) == pole_slot[0]).astype(f32)
    weight = jnp.sum(selector[:, None] * pole_weight, axis=0)
    sign = jnp.where(jnp.arange(2 * B * B) < B * B, -1.0, 1.0).astype(f32)
    weight = jnp.stack([jnp.full((2 * B * B,), weight[0]), sign * weight[1]])
    projector = projector.astype(f32)
    projector = jnp.concatenate([projector, projector], axis=1)
    block, density = products(
        n,
        owners,
        lower.reshape(size, -1),
        trail.reshape(trail.shape[0], -1),
        inverse.reshape(size, -1),
        idx,
        weight,
        projector,
    )
    return block.reshape(1, size, 2, size), density


def solution(mesh):
    in_specs = (
        P("pole", "row", None, "col"),
        P("pole", "col", None, "row"),
        P("pole", "row", None, "col"),
        P(),
        P("pole"),
        P(),
        P(),
        P("pole", None),
    )
    out_specs = (P("pole", "row", None, "col"), P("pole", None))
    return jax.shard_map(local, mesh=mesh, in_specs=in_specs, out_specs=out_specs, check_vma=False)
```

```python
import functools

import jax
import jax.numpy as jnp
from jax import lax
from jax.experimental import pallas as pl
from jax.experimental.pallas import tpu as pltpu
from jax.sharding import PartitionSpec as P

B = 8
HALVES = 4
MESH = pl.DeviceIdType.MESH


def main_kernel(
    n, l_ref, t_ref, inv_ref, idx_ref, weight_ref, proj_ref, block_ref, dens_ref,
    term, pool, coll, slots, term_send, term_recv, coll_send, coll_recv, prod_ref,
    lz, lx, part, own, rs, cz, treal,
    lz_send, lz_recv, lx_send, lx_recv, rs_send, rs_recv, cz_send, cz_recv,
):
    r = lax.axis_index("row")
    c = lax.axis_index("col")
    size = l_ref.shape[0]
    half = size // HALVES
    step = min(128, half)
    width = t_ref.shape[0]
    bf16 = jnp.bfloat16
    f32 = jnp.float32

    barrier = pltpu.get_barrier_semaphore()
    me = lax.axis_index("pole")
    owners = lax.axis_size("pole")
    cells = n * n
    cell = r * n + c

    for j in range(1, n):
        pl.semaphore_signal(barrier, inc=1, device_id={"row": lax.rem(r + j, n)}, device_id_type=MESH)
        pl.semaphore_signal(barrier, inc=1, device_id={"col": lax.rem(c + j, n)}, device_id_type=MESH)
    for j in range(1, owners):
        pl.semaphore_signal(barrier, inc=1, device_id={"pole": lax.rem(me + j, owners)}, device_id_type=MESH)
    pl.semaphore_wait(barrier, 2 * (n - 1) + owners - 1)

    def rows(h):
        return pl.ds(h * half, half)

    def line_copy(src, dst, send, recv, k, h, side):
        to = jnp.maximum(c - 1, 0) if side == 0 else jnp.minimum(c + 1, n - 1)
        return pltpu.make_async_remote_copy(
            src_ref=src,
            dst_ref=dst.at[k, rows(h)],
            send_sem=send.at[side, k, h],
            recv_sem=recv.at[k, h],
            device_id={"col": to},
            device_id_type=MESH,
        )

    def can(side):
        return c > 0 if side == 0 else c < n - 1

    def from_side(side, s):
        k = c + s if side == 0 else c - s
        there = k < n if side == 0 else k >= 0
        return jnp.clip(k, 0, n - 1), there

    def l_copy(k, h, side, mine):
        src = l_ref.at[rows(h)] if mine else lz.at[k, rows(h)]
        return line_copy(src, lz, lz_send, lz_recv, k, h, side)

    def c_copy(k, h, side):
        return line_copy(cz.at[k, rows(h)], cz, cz_send, cz_recv, k, h, side)

    def lx_copy(j):
        return pltpu.make_async_remote_copy(
            src_ref=l_ref,
            dst_ref=lx.at[r],
            send_sem=lx_send.at[j],
            recv_sem=lx_recv.at[r],
            device_id={"row": lax.rem(r + j, n)},
            device_id_type=MESH,
        )

    def lx_wait(j):
        k = lax.rem(r + j, n)
        pltpu.make_async_remote_copy(
            src_ref=l_ref, dst_ref=lx.at[k], send_sem=lx_send.at[j], recv_sem=lx_recv.at[k],
            device_id={"row": k}, device_id_type=MESH,
        ).wait_recv()

    def rs_copy(k, h):
        return pltpu.make_async_remote_copy(
            src_ref=part.at[k, rows(h)],
            dst_ref=rs.at[r, rows(h)],
            send_sem=rs_send.at[k, h],
            recv_sem=rs_recv.at[r, h],
            device_id={"row": k},
            device_id_type=MESH,
        )

    def rs_wait(j, h):
        k = lax.rem(r + j, n)
        pltpu.make_async_remote_copy(
            src_ref=part.at[k, rows(h)], dst_ref=rs.at[k, rows(h)], send_sem=rs_send.at[k, h],
            recv_sem=rs_recv.at[k, h], device_id={"row": k}, device_id_type=MESH,
        ).wait_recv()

    def partial(k, h, mine):
        def one(i, carry):
            at = pl.ds(pl.multiple_of(h * half + i * step, step), step)
            left = l_ref[at] if mine else lz[k, at]
            value = -jnp.dot(left, treal[...], preferred_element_type=f32)

            @pl.when(k == r)
            def _():
                own[at] = value

            @pl.when(k != r)
            def _():
                part[k, at] = value.astype(bf16)

            return carry

        lax.fori_loop(0, half // step, one, 0)

        @pl.when(k != r)
        def _():
            rs_copy(k, h).start()

    def finish():
        for h in range(HALVES):
            for j in range(1, n):
                rs_wait(j, h)

            def one(i, carry):
                at = pl.ds(pl.multiple_of(h * half + i * step, step), step)
                total = own[at]
                for j in range(1, n):
                    total = total + rs[lax.rem(r + j, n), at].astype(f32)
                value = total.astype(bf16)
                cz[c, at] = value
                return carry

            lax.fori_loop(0, half // step, one, 0)
            for side in range(2):
                @pl.when(can(side))
                def _():
                    c_copy(c, h, side).start()

    def accumulate(k, first):
        def with_right(right):
            real = right[:, :width]
            imag = right[:, width:]
            right_re = jnp.concatenate([real, -imag], axis=1)
            right_im = jnp.concatenate([imag, real], axis=1)

            def one(i, carry):
                at = pl.ds(pl.multiple_of(i * step, step), step)
                left = cz[k, at]
                dims = (((1,), (1,)), ((), ()))
                re = lax.dot_general(left, right_re, dims, preferred_element_type=f32)
                im = lax.dot_general(left, right_im, dims, preferred_element_type=f32)
                if first:
                    prod_ref[at, :size] = re
                    prod_ref[at, size:] = im
                else:
                    prod_ref[at, :size] += re
                    prod_ref[at, size:] += im
                return carry

            lax.fori_loop(0, size // step, one, 0)

        @pl.when(k == r)
        def _():
            with_right(l_ref[...])

        @pl.when(k != r)
        def _():
            with_right(lx[k])

    for h in range(HALVES):
        for side in range(2):
            @pl.when(can(side))
            def _():
                l_copy(c, h, side, True).start()

    trail_re = t_ref[:, :width]
    trail_im = t_ref[:, width:]
    treal[:width, :width] = trail_re
    treal[:width, width:] = trail_im
    treal[width:, :width] = -trail_im
    treal[width:, width:] = trail_re
    for h in range(HALVES):
        partial(c, h, True)
    for j in range(1, n):
        lx_copy(j).start()

    per_owner = idx_ref.shape[2]
    most = 2 * per_owner // cells
    held_rows = most * B
    chunk = min(128, held_rows)
    earlier = (
        lax.broadcasted_iota(jnp.int32, (per_owner, per_owner), 0)
        < lax.broadcasted_iota(jnp.int32, (per_owner, per_owner), 1)
    ).astype(f32).astype(bf16)

    def ranks(o):
        cell_of = idx_ref[o, 0:1, :]
        marks = cell_of == lax.broadcasted_iota(jnp.int32, (cells, per_owner), 0).astype(f32)
        marks = jnp.where(marks, 1.0, 0.0)
        before = jnp.dot(marks.astype(bf16), earlier, preferred_element_type=f32)
        return cell_of, jnp.sum(marks * before, axis=0, keepdims=True)

    def index_owner(o, carry):
        cell_of, rank = ranks(o)
        place = jnp.where(cell_of == cell.astype(f32), rank, -1.0)

        def index_chunk(i, inner):
            slot = (lax.broadcasted_iota(jnp.int32, (chunk, per_owner), 0) + i * chunk) >> 3
            pick = jnp.where(place == slot.astype(f32), 1.0, 0.0)
            at = pl.ds(pl.multiple_of(i * chunk, chunk), chunk)
            for v in range(3):
                value = jnp.sum(pick * idx_ref[o, v + 1 : v + 2, :], axis=1, keepdims=True)
                slots[o, v, at] = jnp.broadcast_to(value, (chunk, 128))
            return inner

        lax.fori_loop(0, held_rows // chunk, index_chunk, 0)
        return carry

    lax.fori_loop(0, owners, index_owner, 0)
    apart = jnp.abs(r - c)
    for s in range(1, n):
        for h in range(HALVES):
            for side in range(2):
                k, there = from_side(side, s)

                @pl.when(there)
                def _():
                    l_copy(k, h, side, False).wait_recv()

                    @pl.when(can(side))
                    def _():
                        l_copy(k, h, side, False).start()

            for side in range(2):
                k, there = from_side(side, s)

                @pl.when(there)
                def _():
                    partial(k, h, False)

        if s >= 2:
            @pl.when(apart == s - 2)
            def _():
                finish()

    @pl.when(apart >= n - 2)
    def _():
        finish()

    for j in range(1, n):
        lx_wait(j)
    for t in range(1, n):
        for h in range(HALVES):
            for side in range(2):
                k, there = from_side(side, t)

                @pl.when(there)
                def _():
                    c_copy(k, h, side).wait_recv()

                    @pl.when(can(side))
                    def _():
                        c_copy(k, h, side).start()

        if t == 1:
            accumulate(c, True)
        else:
            for side in range(2):
                k, there = from_side(side, t - 1)

                @pl.when(there)
                def _():
                    accumulate(k, False)

    for side in range(2):
        k, there = from_side(side, n - 1)

        @pl.when(there)
        def _():
            accumulate(k, False)

    def write(i, carry):
        at = pl.ds(pl.multiple_of(i * step, step), step)
        block_ref[at] = (inv_ref[at].astype(f32) - prod_ref[at]).astype(bf16)
        return carry

    lax.fori_loop(0, size // step, write, 0)

    lanes = 2 * B * B
    part_lanes = B * B

    def spread(total, transposed):
        at = lax.broadcasted_iota(jnp.int32, (2 * total, lanes), 0)
        to = lax.broadcasted_iota(jnp.int32, (2 * total, lanes), 1)
        half_of = (at >= total) == (to >= part_lanes)
        inner = ((to & (part_lanes - 1)) >> 3) if transposed else (to & 7)
        return jnp.where(half_of & ((at & 7) == inner), 1.0, 0.0).astype(bf16)

    spread_super = spread(size, False)
    spread_trail = spread(width, True)
    lane = lax.broadcasted_iota(jnp.int32, (chunk, lanes), 1)
    inside = lax.broadcasted_iota(jnp.int32, (chunk, lanes), 0) & 7
    keep_super = ((lane & (part_lanes - 1)) >> 3) == inside
    keep_trail = (lane & 7) == inside
    group = jnp.where(
        lax.broadcasted_iota(jnp.int32, (chunk // B, chunk), 0)
        == (lax.broadcasted_iota(jnp.int32, (chunk // B, chunk), 1) >> 3),
        1.0,
        0.0,
    ).astype(bf16)
    row_of = lax.broadcasted_iota(jnp.int32, (chunk, size), 1).astype(f32)
    row_in = (lax.broadcasted_iota(jnp.int32, (chunk, 1), 0) & 7).astype(f32)
    col_super = lax.broadcasted_iota(jnp.int32, (chunk, 2 * size), 1)
    col_super = jnp.where(col_super >= size, col_super - size, col_super).astype(f32)
    col_trail = lax.broadcasted_iota(jnp.int32, (chunk, 2 * width), 1)
    col_trail = jnp.where(col_trail >= width, col_trail - width, col_trail).astype(f32)
    last = float(B - 1)

    def gather_owner(o, carry):
        def gather_chunk(i, inner):
            at = pl.ds(pl.multiple_of(i * chunk, chunk), chunk)
            first_row = slots[o, 0, at][:, :1]
            first_super = slots[o, 1, at][:, :1]
            first_trail = slots[o, 2, at][:, :1]
            pick = jnp.where(row_of == first_row + row_in, 1.0, 0.0).astype(bf16)
            taken = jnp.dot(pick, block_ref[...], preferred_element_type=f32)
            taken = jnp.where(
                (col_super >= first_super) & (col_super <= first_super + last), taken, 0.0
            ).astype(bf16)
            out_super = jnp.dot(taken, spread_super, preferred_element_type=f32)
            taken = jnp.dot(pick, cz[c], preferred_element_type=f32)
            taken = jnp.where(
                (col_trail >= first_trail) & (col_trail <= first_trail + last), taken, 0.0
            ).astype(bf16)
            out_trail = jnp.dot(taken, spread_trail, preferred_element_type=f32)
            both = jnp.where(keep_super, out_super, 0.0) + jnp.where(keep_trail, out_trail, 0.0)
            value = jnp.dot(group, both.astype(bf16), preferred_element_type=f32)
            swapped = jnp.concatenate([value[:, part_lanes:], value[:, :part_lanes]], axis=1)
            to = pl.ds(pl.multiple_of(i * (chunk // B), chunk // B), chunk // B)
            term[o, to] = weight_ref[0:1] * value + weight_ref[1:2] * swapped
            return inner

        lax.fori_loop(0, held_rows // chunk, gather_chunk, 0)
        return carry

    lax.fori_loop(0, owners, gather_owner, 0)

    def term_copy(j):
        to = lax.rem(me + j, owners)
        return pltpu.make_async_remote_copy(
            src_ref=term.at[to], dst_ref=pool.at[j], send_sem=term_send.at[j],
            recv_sem=term_recv.at[j], device_id={"pole": to}, device_id_type=MESH,
        )

    for j in range(1, owners):
        term_copy(j).start()
    for j in range(1, owners):
        term_copy(j).wait_recv()
    total = term[me]
    for j in range(1, owners):
        total = total + pool[j]
    coll[cell] = total

    def coll_copy(j, at_col):
        at = r * n + at_col
        return pltpu.make_async_remote_copy(
            src_ref=coll.at[at], dst_ref=coll.at[at], send_sem=coll_send.at[j],
            recv_sem=coll_recv.at[at_col], device_id={"col": lax.rem(c + j, n)}, device_id_type=MESH,
        )

    def group_copy(j, at_row):
        at = pl.ds(at_row * n, n)
        return pltpu.make_async_remote_copy(
            src_ref=coll.at[at], dst_ref=coll.at[at], send_sem=coll_send.at[n + j],
            recv_sem=coll_recv.at[n + at_row], device_id={"row": lax.rem(r + j, n)}, device_id_type=MESH,
        )

    for j in range(1, n):
        coll_copy(j, c).start()
    cell_of, rank = ranks(me)
    target = jnp.broadcast_to(cell_of * most + rank, (128, per_owner))
    target = jnp.transpose(target)
    for j in range(1, n):
        coll_copy(j, lax.rem(c + j, n)).wait_recv()
    for j in range(1, n):
        group_copy(j, r).start()
    for j in range(1, n):
        group_copy(j, lax.rem(r + j, n)).wait_recv()
    for q in range(per_owner // 128):
        mine = target[q * 128 : (q + 1) * 128, :1]
        pick = jnp.where(
            mine == lax.broadcasted_iota(jnp.int32, (128, cells * most), 1).astype(f32), 1.0, 0.0
        ).astype(bf16)
        rest = coll[...].reshape(cells * most, lanes)
        summed = jnp.zeros((128, lanes), f32)
        for _ in range(3):
            top = rest.astype(bf16)
            rest = rest - top.astype(f32)
            summed = summed + jnp.dot(pick, top, preferred_element_type=f32)
        dens_ref[q * 128 : (q + 1) * 128] = summed * proj_ref[q * 128 : (q + 1) * 128]

    for j in range(1, owners):
        term_copy(j).wait_send()
    for j in range(1, n):
        coll_copy(j, c).wait_send()
        group_copy(j, r).wait_send()
    for j in range(1, n):
        lx_copy(j).wait_send()
        for h in range(HALVES):
            rs_copy(lax.rem(r + j, n), h).wait_send()
    for s in range(n):
        for h in range(HALVES):
            for side in range(2):
                k, there = from_side(side, s)

                @pl.when(there & can(side))
                def _():
                    l_copy(k, h, side, s == 0).wait_send()
                    c_copy(k, h, side).wait_send()


def products(n, owners, lower, trail, inverse, idx, weight, projector):
    size = lower.shape[0]
    wide = lower.shape[1]
    bf16 = jnp.bfloat16
    lanes = 2 * B * B
    most = 2 * idx.shape[2] // (n * n)
    dma = pltpu.SemaphoreType.DMA
    vmem = pl.BlockSpec(memory_space=pltpu.VMEM)
    return pl.pallas_call(
        functools.partial(main_kernel, n),
        name="products",
        out_shape=(
            jax.ShapeDtypeStruct((size, 2 * size), bf16),
            jax.ShapeDtypeStruct(projector.shape, jnp.float32),
        ),
        in_specs=[vmem] * 6,
        out_specs=(vmem, vmem),
        scratch_shapes=[
            pltpu.VMEM((owners, most, lanes), jnp.float32),
            pltpu.VMEM((owners, most, lanes), jnp.float32),
            pltpu.VMEM((n * n, most, lanes), jnp.float32),
            pltpu.VMEM((owners, 3, most * B, 128), jnp.float32),
            dma((owners,)),
            dma((owners,)),
            dma((2 * n,)),
            dma((2 * n,)),
            pltpu.VMEM((size, 2 * size), jnp.float32),
            pltpu.VMEM((n, size, wide), bf16),
            pltpu.VMEM((n, size, wide), bf16),
            pltpu.VMEM((n, size, wide), bf16),
            pltpu.VMEM((size, wide), jnp.float32),
            pltpu.VMEM((n, size, wide), bf16),
            pltpu.VMEM((n, size, wide), bf16),
            pltpu.VMEM((wide, wide), bf16),
            dma((2, n, HALVES)),
            dma((n, HALVES)),
            dma((n,)),
            dma((n,)),
            dma((n, HALVES)),
            dma((n, HALVES)),
            dma((2, n, HALVES)),
            dma((n, HALVES)),
        ],
        compiler_params=pltpu.CompilerParams(
            collective_id=0, has_side_effects=True, vmem_limit_bytes=40 * 1024 * 1024
        ),
    )(lower, trail, inverse, idx, weight, projector)


def local(
    inverse_trail, lower_t, diag_inverse, pole_weight, pole_slot, pair_row, pair_col, projector
):
    trail = inverse_trail[0]
    lower = lower_t[0]
    inverse = diag_inverse[0]
    n = lax.axis_size("row")
    owners = lax.axis_size("pole")
    f32 = jnp.float32
    size = lower.shape[0]
    atoms = size // B
    trail_atoms = trail.shape[2] // B
    in_super = pair_row < atoms * n
    trail_atom = jnp.maximum(pair_row - atoms * n, 0)
    row_atom = jnp.where(in_super, pair_row, pair_col)
    col_atom = jnp.where(in_super, pair_col, trail_atom)
    cell_row = row_atom // atoms
    cell_col = jnp.where(in_super, col_atom // atoms, col_atom // trail_atoms)
    away = -8 * size
    row_first = (row_atom - cell_row * atoms) * B
    super_first = jnp.where(in_super, (col_atom - cell_col * atoms) * B, away)
    trail_first = jnp.where(in_super, away, (col_atom - cell_col * trail_atoms) * B)
    idx = jnp.stack(
        [
            x.reshape(owners, -1).astype(f32)
            for x in (cell_row * n + cell_col, row_first, super_first, trail_first)
        ],
        axis=1,
    )
    selector = (jnp.arange(pole_weight.shape[0], dtype=jnp.int32) == pole_slot[0]).astype(f32)
    weight = jnp.sum(selector[:, None] * pole_weight, axis=0)
    sign = jnp.where(jnp.arange(2 * B * B) < B * B, -1.0, 1.0).astype(f32)
    weight = jnp.stack([jnp.full((2 * B * B,), weight[0]), sign * weight[1]])
    projector = projector.astype(f32)
    projector = jnp.concatenate([projector, projector], axis=1)
    block, density = products(
        n,
        owners,
        lower.reshape(size, -1),
        trail.reshape(trail.shape[0], -1),
        inverse.reshape(size, -1),
        idx,
        weight,
        projector,
    )
    return block.reshape(1, size, 2, size), density


def solution(mesh):
    in_specs = (
        P("pole", "row", None, "col"),
        P("pole", "col", None, "row"),
        P("pole", "row", None, "col"),
        P(),
        P("pole"),
        P(),
        P(),
        P("pole", None),
    )
    out_specs = (P("pole", "row", None, "col"), P("pole", None))
    return jax.shard_map(local, mesh=mesh, in_specs=in_specs, out_specs=out_specs, check_vma=False)
```

```python
import functools

import jax
import jax.numpy as jnp
from jax import lax
from jax.experimental import pallas as pl
from jax.experimental.pallas import tpu as pltpu
from jax.sharding import PartitionSpec as P

B = 8
HALVES = 4
MESH = pl.DeviceIdType.MESH


def main_kernel(
    n, l_ref, t_ref, inv_ref, prow_ref, pcol_ref, table_ref, slot_ref, proj_ref, block_ref, dens_ref,
    idx_ref, weight_ref, term, pool, coll, slots, term_send, term_recv, coll_send, coll_recv, prod_ref,
    lz, lx, part, own, rs, cz, treal,
    lz_send, lz_recv, lx_send, lx_recv, rs_send, rs_recv, cz_send, cz_recv,
):
    r = lax.axis_index("row")
    c = lax.axis_index("col")
    size = l_ref.shape[0]
    half = size // HALVES
    step = min(128, half)
    width = t_ref.shape[0]
    bf16 = jnp.bfloat16
    f32 = jnp.float32

    barrier = pltpu.get_barrier_semaphore()
    me = lax.axis_index("pole")
    owners = lax.axis_size("pole")
    cells = n * n
    cell = r * n + c

    for j in range(1, n):
        pl.semaphore_signal(barrier, inc=1, device_id={"row": lax.rem(r + j, n)}, device_id_type=MESH)
        pl.semaphore_signal(barrier, inc=1, device_id={"col": lax.rem(c + j, n)}, device_id_type=MESH)
    for j in range(1, owners):
        pl.semaphore_signal(barrier, inc=1, device_id={"pole": lax.rem(me + j, owners)}, device_id_type=MESH)
    pl.semaphore_wait(barrier, 2 * (n - 1) + owners - 1)

    def rows(h):
        return pl.ds(h * half, half)

    def line_copy(src, dst, send, recv, k, h, side):
        to = jnp.maximum(c - 1, 0) if side == 0 else jnp.minimum(c + 1, n - 1)
        return pltpu.make_async_remote_copy(
            src_ref=src,
            dst_ref=dst.at[k, rows(h)],
            send_sem=send.at[side, k, h],
            recv_sem=recv.at[k, h],
            device_id={"col": to},
            device_id_type=MESH,
        )

    def can(side):
        return c > 0 if side == 0 else c < n - 1

    def from_side(side, s):
        k = c + s if side == 0 else c - s
        there = k < n if side == 0 else k >= 0
        return jnp.clip(k, 0, n - 1), there

    def l_copy(k, h, side, mine):
        src = l_ref.at[rows(h)] if mine else lz.at[k, rows(h)]
        return line_copy(src, lz, lz_send, lz_recv, k, h, side)

    def c_copy(k, h, side):
        return line_copy(cz.at[k, rows(h)], cz, cz_send, cz_recv, k, h, side)

    def lx_copy(j):
        return pltpu.make_async_remote_copy(
            src_ref=l_ref,
            dst_ref=lx.at[r],
            send_sem=lx_send.at[j],
            recv_sem=lx_recv.at[r],
            device_id={"row": lax.rem(r + j, n)},
            device_id_type=MESH,
        )

    def lx_wait(j):
        k = lax.rem(r + j, n)
        pltpu.make_async_remote_copy(
            src_ref=l_ref, dst_ref=lx.at[k], send_sem=lx_send.at[j], recv_sem=lx_recv.at[k],
            device_id={"row": k}, device_id_type=MESH,
        ).wait_recv()

    def rs_copy(k, h):
        return pltpu.make_async_remote_copy(
            src_ref=part.at[k, rows(h)],
            dst_ref=rs.at[r, rows(h)],
            send_sem=rs_send.at[k, h],
            recv_sem=rs_recv.at[r, h],
            device_id={"row": k},
            device_id_type=MESH,
        )

    def rs_wait(j, h):
        k = lax.rem(r + j, n)
        pltpu.make_async_remote_copy(
            src_ref=part.at[k, rows(h)], dst_ref=rs.at[k, rows(h)], send_sem=rs_send.at[k, h],
            recv_sem=rs_recv.at[k, h], device_id={"row": k}, device_id_type=MESH,
        ).wait_recv()

    def partial(k, h, mine):
        def one(i, carry):
            at = pl.ds(pl.multiple_of(h * half + i * step, step), step)
            left = l_ref[at] if mine else lz[k, at]
            value = -jnp.dot(left, treal[...], preferred_element_type=f32)

            @pl.when(k == r)
            def _():
                own[at] = value

            @pl.when(k != r)
            def _():
                part[k, at] = value.astype(bf16)

            return carry

        lax.fori_loop(0, half // step, one, 0)

        @pl.when(k != r)
        def _():
            rs_copy(k, h).start()

    def finish():
        for h in range(HALVES):
            for j in range(1, n):
                rs_wait(j, h)

            def one(i, carry):
                at = pl.ds(pl.multiple_of(h * half + i * step, step), step)
                total = own[at]
                for j in range(1, n):
                    total = total + rs[lax.rem(r + j, n), at].astype(f32)
                value = total.astype(bf16)
                cz[c, at] = value
                return carry

            lax.fori_loop(0, half // step, one, 0)
            for side in range(2):
                @pl.when(can(side))
                def _():
                    c_copy(c, h, side).start()

    def accumulate(k, first):
        def with_right(right):
            real = right[:, :width]
            imag = right[:, width:]
            right_re = jnp.concatenate([real, -imag], axis=1)
            right_im = jnp.concatenate([imag, real], axis=1)

            def one(i, carry):
                at = pl.ds(pl.multiple_of(i * step, step), step)
                left = cz[k, at]
                dims = (((1,), (1,)), ((), ()))
                re = lax.dot_general(left, right_re, dims, preferred_element_type=f32)
                im = lax.dot_general(left, right_im, dims, preferred_element_type=f32)
                if first:
                    prod_ref[at, :size] = re
                    prod_ref[at, size:] = im
                else:
                    prod_ref[at, :size] += re
                    prod_ref[at, size:] += im
                return carry

            lax.fori_loop(0, size // step, one, 0)

        @pl.when(k == r)
        def _():
            with_right(l_ref[...])

        @pl.when(k != r)
        def _():
            with_right(lx[k])

    for h in range(HALVES):
        for side in range(2):
            @pl.when(can(side))
            def _():
                l_copy(c, h, side, True).start()

    trail_re = t_ref[:, :width]
    trail_im = t_ref[:, width:]
    treal[:width, :width] = trail_re
    treal[:width, width:] = trail_im
    treal[width:, :width] = -trail_im
    treal[width:, width:] = trail_re
    for h in range(HALVES):
        partial(c, h, True)
    for j in range(1, n):
        lx_copy(j).start()

    atoms = size // B
    trail_atoms = width // B

    def split(value, by):
        whole = jnp.floor((value + 0.5) * (1.0 / by))
        return whole, value - whole * by

    pair_row = prow_ref[...].astype(f32)
    pair_col = pcol_ref[...].astype(f32)
    in_super = pair_row < float(atoms * n)
    trail_atom = jnp.maximum(pair_row - float(atoms * n), 0.0)
    cell_row, row_in_cell = split(jnp.where(in_super, pair_row, pair_col), atoms)
    col_super, super_in_cell = split(pair_col, atoms)
    col_trail, trail_in_cell = split(trail_atom, trail_atoms)
    away = float(-8 * size)
    idx_ref[:, 0] = cell_row * n + jnp.where(in_super, col_super, col_trail)
    idx_ref[:, 1] = row_in_cell * B
    idx_ref[:, 2] = jnp.where(in_super, super_in_cell * B, away)
    idx_ref[:, 3] = jnp.where(in_super, away, trail_in_cell * B)
    table = table_ref[...]
    chosen = lax.broadcasted_iota(jnp.int32, table.shape, 0) == slot_ref[0]
    chosen = jnp.sum(jnp.where(chosen, table, 0.0), axis=0, keepdims=True)
    all_lanes = lax.broadcasted_iota(jnp.int32, (1, 2 * B * B), 1)
    weight_ref[0:1] = jnp.broadcast_to(chosen[:, 0:1], (1, 2 * B * B))
    weight_ref[1:2] = jnp.where(all_lanes < B * B, -1.0, 1.0) * chosen[:, 1:2]
    per_owner = idx_ref.shape[2]
    most = 2 * per_owner // cells
    held_rows = most * B
    chunk = min(128, held_rows)
    earlier = (
        lax.broadcasted_iota(jnp.int32, (per_owner, per_owner), 0)
        < lax.broadcasted_iota(jnp.int32, (per_owner, per_owner), 1)
    ).astype(f32).astype(bf16)

    def ranks(o):
        cell_of = idx_ref[o, 0:1, :]
        marks = cell_of == lax.broadcasted_iota(jnp.int32, (cells, per_owner), 0).astype(f32)
        marks = jnp.where(marks, 1.0, 0.0)
        before = jnp.dot(marks.astype(bf16), earlier, preferred_element_type=f32)
        return cell_of, jnp.sum(marks * before, axis=0, keepdims=True)

    def index_owner(o, carry):
        cell_of, rank = ranks(o)
        place = jnp.where(cell_of == cell.astype(f32), rank, -1.0)

        def index_chunk(i, inner):
            slot = (lax.broadcasted_iota(jnp.int32, (chunk, per_owner), 0) + i * chunk) >> 3
            pick = jnp.where(place == slot.astype(f32), 1.0, 0.0)
            at = pl.ds(pl.multiple_of(i * chunk, chunk), chunk)
            for v in range(3):
                value = jnp.sum(pick * idx_ref[o, v + 1 : v + 2, :], axis=1, keepdims=True)
                slots[o, v, at] = jnp.broadcast_to(value, (chunk, 128))
            return inner

        lax.fori_loop(0, held_rows // chunk, index_chunk, 0)
        return carry

    lax.fori_loop(0, owners, index_owner, 0)
    apart = jnp.abs(r - c)
    for s in range(1, n):
        for h in range(HALVES):
            for side in range(2):
                k, there = from_side(side, s)

                @pl.when(there)
                def _():
                    l_copy(k, h, side, False).wait_recv()

                    @pl.when(can(side))
                    def _():
                        l_copy(k, h, side, False).start()

            for side in range(2):
                k, there = from_side(side, s)

                @pl.when(there)
                def _():
                    partial(k, h, False)

        if s >= 2:
            @pl.when(apart == s - 2)
            def _():
                finish()

    @pl.when(apart >= n - 2)
    def _():
        finish()

    lanes = 2 * B * B
    part_lanes = B * B

    def spread(total, transposed):
        at = lax.broadcasted_iota(jnp.int32, (2 * total, lanes), 0)
        to = lax.broadcasted_iota(jnp.int32, (2 * total, lanes), 1)
        half_of = (at >= total) == (to >= part_lanes)
        inner = ((to & (part_lanes - 1)) >> 3) if transposed else (to & 7)
        return jnp.where(half_of & ((at & 7) == inner), 1.0, 0.0).astype(bf16)

    spread_super = spread(size, False)
    spread_trail = spread(width, True)
    lane = lax.broadcasted_iota(jnp.int32, (chunk, lanes), 1)
    inside = lax.broadcasted_iota(jnp.int32, (chunk, lanes), 0) & 7
    keep_super = ((lane & (part_lanes - 1)) >> 3) == inside
    keep_trail = (lane & 7) == inside
    group = jnp.where(
        lax.broadcasted_iota(jnp.int32, (chunk // B, chunk), 0)
        == (lax.broadcasted_iota(jnp.int32, (chunk // B, chunk), 1) >> 3),
        1.0,
        0.0,
    ).astype(bf16)
    row_of = lax.broadcasted_iota(jnp.int32, (chunk, size), 1).astype(f32)
    row_in = (lax.broadcasted_iota(jnp.int32, (chunk, 1), 0) & 7).astype(f32)
    col_super = lax.broadcasted_iota(jnp.int32, (chunk, 2 * size), 1)
    col_super = jnp.where(col_super >= size, col_super - size, col_super).astype(f32)
    col_trail = lax.broadcasted_iota(jnp.int32, (chunk, 2 * width), 1)
    col_trail = jnp.where(col_trail >= width, col_trail - width, col_trail).astype(f32)
    last = float(B - 1)

    def trail_owner(o, carry):
        def trail_chunk(i, inner):
            at = pl.ds(pl.multiple_of(i * chunk, chunk), chunk)
            first_row = slots[o, 0, at][:, :1]
            first_trail = slots[o, 2, at][:, :1]
            pick = jnp.where(row_of == first_row + row_in, 1.0, 0.0).astype(bf16)
            taken = jnp.dot(pick, cz[c], preferred_element_type=f32)
            taken = jnp.where(
                (col_trail >= first_trail) & (col_trail <= first_trail + last), taken, 0.0
            ).astype(bf16)
            out_trail = jnp.dot(taken, spread_trail, preferred_element_type=f32)
            slots[o, 2, at] = jnp.where(keep_trail, out_trail, 0.0)
            return inner

        lax.fori_loop(0, held_rows // chunk, trail_chunk, 0)
        return carry

    for j in range(1, n):
        lx_wait(j)
    for t in range(1, n):
        for h in range(HALVES):
            for side in range(2):
                k, there = from_side(side, t)

                @pl.when(there)
                def _():
                    c_copy(k, h, side).wait_recv()

                    @pl.when(can(side))
                    def _():
                        c_copy(k, h, side).start()

        if t == 1:
            accumulate(c, True)
            lax.fori_loop(0, owners, trail_owner, 0)
        else:
            for side in range(2):
                k, there = from_side(side, t - 1)

                @pl.when(there)
                def _():
                    accumulate(k, False)

    for side in range(2):
        k, there = from_side(side, n - 1)

        @pl.when(there)
        def _():
            accumulate(k, False)

    def write(i, carry):
        at = pl.ds(pl.multiple_of(i * step, step), step)
        block_ref[at] = (inv_ref[at].astype(f32) - prod_ref[at]).astype(bf16)
        return carry

    lax.fori_loop(0, size // step, write, 0)

    def gather_owner(o, carry):
        def gather_chunk(i, inner):
            at = pl.ds(pl.multiple_of(i * chunk, chunk), chunk)
            first_row = slots[o, 0, at][:, :1]
            first_super = slots[o, 1, at][:, :1]
            pick = jnp.where(row_of == first_row + row_in, 1.0, 0.0).astype(bf16)
            taken = jnp.dot(pick, block_ref[...], preferred_element_type=f32)
            taken = jnp.where(
                (col_super >= first_super) & (col_super <= first_super + last), taken, 0.0
            ).astype(bf16)
            out_super = jnp.dot(taken, spread_super, preferred_element_type=f32)
            both = jnp.where(keep_super, out_super, 0.0) + slots[o, 2, at]
            value = jnp.dot(group, both.astype(bf16), preferred_element_type=f32)
            swapped = jnp.concatenate([value[:, part_lanes:], value[:, :part_lanes]], axis=1)
            to = pl.ds(pl.multiple_of(i * (chunk // B), chunk // B), chunk // B)
            term[o, to] = weight_ref[0:1] * value + weight_ref[1:2] * swapped
            return inner

        lax.fori_loop(0, held_rows // chunk, gather_chunk, 0)
        return carry

    def term_copy(j):
        to = lax.rem(me + j, owners)
        return pltpu.make_async_remote_copy(
            src_ref=term.at[to], dst_ref=pool.at[j], send_sem=term_send.at[j],
            recv_sem=term_recv.at[j], device_id={"pole": to}, device_id_type=MESH,
        )

    for j in range(1, owners):
        gather_owner(lax.rem(me + j, owners), 0)
        term_copy(j).start()
    gather_owner(me, 0)
    for j in range(1, owners):
        term_copy(j).wait_recv()
    total = term[me]
    for j in range(1, owners):
        total = total + pool[j]
    coll[cell] = total

    def coll_copy(j, at_col):
        at = r * n + at_col
        return pltpu.make_async_remote_copy(
            src_ref=coll.at[at], dst_ref=coll.at[at], send_sem=coll_send.at[j],
            recv_sem=coll_recv.at[at_col], device_id={"col": lax.rem(c + j, n)}, device_id_type=MESH,
        )

    def group_copy(j, at_row):
        at = pl.ds(at_row * n, n)
        return pltpu.make_async_remote_copy(
            src_ref=coll.at[at], dst_ref=coll.at[at], send_sem=coll_send.at[n + j],
            recv_sem=coll_recv.at[n + at_row], device_id={"row": lax.rem(r + j, n)}, device_id_type=MESH,
        )

    for j in range(1, n):
        coll_copy(j, c).start()
    cell_of, rank = ranks(me)
    target = jnp.broadcast_to(cell_of * most + rank, (128, per_owner))
    target = jnp.transpose(target)
    for j in range(1, n):
        coll_copy(j, lax.rem(c + j, n)).wait_recv()
    for j in range(1, n):
        group_copy(j, r).start()
    for j in range(1, n):
        group_copy(j, lax.rem(r + j, n)).wait_recv()
    for q in range(per_owner // 128):
        mine = target[q * 128 : (q + 1) * 128, :1]
        pick = jnp.where(
            mine == lax.broadcasted_iota(jnp.int32, (128, cells * most), 1).astype(f32), 1.0, 0.0
        ).astype(bf16)
        rest = coll[...].reshape(cells * most, lanes)
        summed = jnp.zeros((128, lanes), f32)
        for _ in range(3):
            top = rest.astype(bf16)
            rest = rest - top.astype(f32)
            summed = summed + jnp.dot(pick, top, preferred_element_type=f32)
        mine = proj_ref[q * 128 : (q + 1) * 128].astype(f32)
        dens_ref[q * 128 : (q + 1) * 128] = summed * jnp.concatenate([mine, mine], axis=1)

    for j in range(1, owners):
        term_copy(j).wait_send()
    for j in range(1, n):
        coll_copy(j, c).wait_send()
        group_copy(j, r).wait_send()
    for j in range(1, n):
        lx_copy(j).wait_send()
        for h in range(HALVES):
            rs_copy(lax.rem(r + j, n), h).wait_send()
    for s in range(n):
        for h in range(HALVES):
            for side in range(2):
                k, there = from_side(side, s)

                @pl.when(there & can(side))
                def _():
                    l_copy(k, h, side, s == 0).wait_send()
                    c_copy(k, h, side).wait_send()


def products(n, owners, lower, trail, inverse, pair_row, pair_col, table, slot, projector):
    size = lower.shape[0]
    wide = lower.shape[1]
    bf16 = jnp.bfloat16
    lanes = 2 * B * B
    per_owner = projector.shape[0]
    most = 2 * per_owner // (n * n)
    dma = pltpu.SemaphoreType.DMA
    vmem = pl.BlockSpec(memory_space=pltpu.VMEM)
    return pl.pallas_call(
        functools.partial(main_kernel, n),
        name="products",
        out_shape=(
            jax.ShapeDtypeStruct((size, 2 * size), bf16),
            jax.ShapeDtypeStruct((per_owner, lanes), jnp.float32),
        ),
        in_specs=[vmem] * 6 + [pl.BlockSpec(memory_space=pltpu.SMEM), vmem],
        out_specs=(vmem, vmem),
        scratch_shapes=[
            pltpu.VMEM((owners, 4, per_owner), jnp.float32),
            pltpu.VMEM((2, lanes), jnp.float32),
            pltpu.VMEM((owners, most, lanes), jnp.float32),
            pltpu.VMEM((owners, most, lanes), jnp.float32),
            pltpu.VMEM((n * n, most, lanes), jnp.float32),
            pltpu.VMEM((owners, 3, most * B, 128), jnp.float32),
            dma((owners,)),
            dma((owners,)),
            dma((2 * n,)),
            dma((2 * n,)),
            pltpu.VMEM((size, 2 * size), jnp.float32),
            pltpu.VMEM((n, size, wide), bf16),
            pltpu.VMEM((n, size, wide), bf16),
            pltpu.VMEM((n, size, wide), bf16),
            pltpu.VMEM((size, wide), jnp.float32),
            pltpu.VMEM((n, size, wide), bf16),
            pltpu.VMEM((n, size, wide), bf16),
            pltpu.VMEM((wide, wide), bf16),
            dma((2, n, HALVES)),
            dma((n, HALVES)),
            dma((n,)),
            dma((n,)),
            dma((n, HALVES)),
            dma((n, HALVES)),
            dma((2, n, HALVES)),
            dma((n, HALVES)),
        ],
        compiler_params=pltpu.CompilerParams(
            collective_id=0, has_side_effects=True, vmem_limit_bytes=40 * 1024 * 1024
        ),
    )(lower, trail, inverse, pair_row, pair_col, table, slot, projector)


def local(
    inverse_trail, lower_t, diag_inverse, pole_weight, pole_slot, pair_row, pair_col, projector
):
    trail = inverse_trail[0]
    lower = lower_t[0]
    inverse = diag_inverse[0]
    n = lax.axis_size("row")
    owners = lax.axis_size("pole")
    size = lower.shape[0]
    block, density = products(
        n,
        owners,
        lower.reshape(size, -1),
        trail.reshape(trail.shape[0], -1),
        inverse.reshape(size, -1),
        pair_row.reshape(owners, -1),
        pair_col.reshape(owners, -1),
        pole_weight,
        pole_slot,
        projector,
    )
    return block.reshape(1, size, 2, size), density


def solution(mesh):
    in_specs = (
        P("pole", "row", None, "col"),
        P("pole", "col", None, "row"),
        P("pole", "row", None, "col"),
        P(),
        P("pole"),
        P(),
        P(),
        P("pole", None),
    )
    out_specs = (P("pole", "row", None, "col"), P("pole", None))
    return jax.shard_map(local, mesh=mesh, in_specs=in_specs, out_specs=out_specs, check_vma=False)
```

```python
import functools

import jax
import jax.numpy as jnp
from jax import lax
from jax.experimental import pallas as pl
from jax.experimental.pallas import tpu as pltpu
from jax.sharding import PartitionSpec as P

B = 8
HALVES = 4
MESH = pl.DeviceIdType.MESH


def main_kernel(
    n, l_ref, t_ref, inv_ref, prow_ref, pcol_ref, table_ref, slot_ref, proj_ref, block_ref, dens_ref,
    idx_ref, weight_ref, term, pool, coll, slots, term_send, term_recv, coll_send, coll_recv, prod_ref,
    lz, lx, part, own, rs, cz, treal,
    lz_send, lz_recv, lx_send, lx_recv, rs_send, rs_recv, cz_send, cz_recv,
):
    r = lax.axis_index("row")
    c = lax.axis_index("col")
    size = l_ref.shape[0]
    half = size // HALVES
    step = min(128, half)
    width = t_ref.shape[0]
    bf16 = jnp.bfloat16
    f32 = jnp.float32

    barrier = pltpu.get_barrier_semaphore()
    me = lax.axis_index("pole")
    owners = lax.axis_size("pole")
    cells = n * n
    cell = r * n + c

    for j in range(1, n):
        pl.semaphore_signal(barrier, inc=1, device_id={"row": lax.rem(r + j, n)}, device_id_type=MESH)
        pl.semaphore_signal(barrier, inc=1, device_id={"col": lax.rem(c + j, n)}, device_id_type=MESH)
    for j in range(1, owners):
        pl.semaphore_signal(barrier, inc=1, device_id={"pole": lax.rem(me + j, owners)}, device_id_type=MESH)
    pl.semaphore_wait(barrier, 2 * (n - 1) + owners - 1)

    def rows(h):
        return pl.ds(h * half, half)

    def line_copy(src, dst, send, recv, k, h, side):
        to = jnp.maximum(c - 1, 0) if side == 0 else jnp.minimum(c + 1, n - 1)
        return pltpu.make_async_remote_copy(
            src_ref=src,
            dst_ref=dst.at[k, rows(h)],
            send_sem=send.at[side, k, h],
            recv_sem=recv.at[k, h],
            device_id={"col": to},
            device_id_type=MESH,
        )

    def can(side):
        return c > 0 if side == 0 else c < n - 1

    def from_side(side, s):
        k = c + s if side == 0 else c - s
        there = k < n if side == 0 else k >= 0
        return jnp.clip(k, 0, n - 1), there

    def l_copy(k, h, side, mine):
        src = l_ref.at[rows(h)] if mine else lz.at[k, rows(h)]
        return line_copy(src, lz, lz_send, lz_recv, k, h, side)

    def c_copy(k, h, side):
        return line_copy(cz.at[k, rows(h)], cz, cz_send, cz_recv, k, h, side)

    def lx_copy(j):
        return pltpu.make_async_remote_copy(
            src_ref=l_ref,
            dst_ref=lx.at[r],
            send_sem=lx_send.at[j],
            recv_sem=lx_recv.at[r],
            device_id={"row": lax.rem(r + j, n)},
            device_id_type=MESH,
        )

    def lx_wait(j):
        k = lax.rem(r + j, n)
        pltpu.make_async_remote_copy(
            src_ref=l_ref, dst_ref=lx.at[k], send_sem=lx_send.at[j], recv_sem=lx_recv.at[k],
            device_id={"row": k}, device_id_type=MESH,
        ).wait_recv()

    def rs_copy(k, h):
        return pltpu.make_async_remote_copy(
            src_ref=part.at[k, rows(h)],
            dst_ref=rs.at[r, rows(h)],
            send_sem=rs_send.at[k, h],
            recv_sem=rs_recv.at[r, h],
            device_id={"row": k},
            device_id_type=MESH,
        )

    def rs_wait(j, h):
        k = lax.rem(r + j, n)
        pltpu.make_async_remote_copy(
            src_ref=part.at[k, rows(h)], dst_ref=rs.at[k, rows(h)], send_sem=rs_send.at[k, h],
            recv_sem=rs_recv.at[k, h], device_id={"row": k}, device_id_type=MESH,
        ).wait_recv()

    def partial(k, h, mine):
        def one(i, carry):
            at = pl.ds(pl.multiple_of(h * half + i * step, step), step)
            left = l_ref[at] if mine else lz[k, at]
            value = -jnp.dot(left, treal[...], preferred_element_type=f32)

            @pl.when(k == r)
            def _():
                own[at] = value

            @pl.when(k != r)
            def _():
                part[k, at] = value.astype(bf16)

            return carry

        lax.fori_loop(0, half // step, one, 0)

        @pl.when(k != r)
        def _():
            rs_copy(k, h).start()

    def finish():
        for h in range(HALVES):
            for j in range(1, n):
                rs_wait(j, h)

            def one(i, carry):
                at = pl.ds(pl.multiple_of(h * half + i * step, step), step)
                total = own[at]
                for j in range(1, n):
                    total = total + rs[lax.rem(r + j, n), at].astype(f32)
                value = total.astype(bf16)
                cz[c, at] = value
                return carry

            lax.fori_loop(0, half // step, one, 0)
            for side in range(2):
                @pl.when(can(side))
                def _():
                    c_copy(c, h, side).start()

    def accumulate(k, first):
        def with_right(right):
            real = right[:, :width]
            imag = right[:, width:]
            right_re = jnp.concatenate([real, -imag], axis=1)
            right_im = jnp.concatenate([imag, real], axis=1)

            def one(i, carry):
                at = pl.ds(pl.multiple_of(i * step, step), step)
                left = cz[k, at]
                dims = (((1,), (1,)), ((), ()))
                re = lax.dot_general(left, right_re, dims, preferred_element_type=f32)
                im = lax.dot_general(left, right_im, dims, preferred_element_type=f32)
                if first:
                    prod_ref[at, :size] = re
                    prod_ref[at, size:] = im
                else:
                    prod_ref[at, :size] += re
                    prod_ref[at, size:] += im
                return carry

            lax.fori_loop(0, size // step, one, 0)

        @pl.when(k == r)
        def _():
            with_right(l_ref[...])

        @pl.when(k != r)
        def _():
            with_right(lx[k])

    for h in range(HALVES):
        for side in range(2):
            @pl.when(can(side))
            def _():
                l_copy(c, h, side, True).start()

    trail_re = t_ref[:, :width]
    trail_im = t_ref[:, width:]
    treal[:width, :width] = trail_re
    treal[:width, width:] = trail_im
    treal[width:, :width] = -trail_im
    treal[width:, width:] = trail_re
    for h in range(HALVES):
        partial(c, h, True)
    for j in range(1, n):
        lx_copy(j).start()

    atoms = size // B
    trail_atoms = width // B

    def split(value, by):
        whole = jnp.floor((value + 0.5) * (1.0 / by))
        return whole, value - whole * by

    pair_row = prow_ref[...].astype(f32)
    pair_col = pcol_ref[...].astype(f32)
    in_super = pair_row < float(atoms * n)
    trail_atom = jnp.maximum(pair_row - float(atoms * n), 0.0)
    cell_row, row_in_cell = split(jnp.where(in_super, pair_row, pair_col), atoms)
    col_super, super_in_cell = split(pair_col, atoms)
    col_trail, trail_in_cell = split(trail_atom, trail_atoms)
    away = float(-8 * size)
    idx_ref[:, 0] = cell_row * n + jnp.where(in_super, col_super, col_trail)
    idx_ref[:, 1] = row_in_cell * B
    idx_ref[:, 2] = jnp.where(in_super, super_in_cell * B, away)
    idx_ref[:, 3] = jnp.where(in_super, away, trail_in_cell * B)
    table = table_ref[...]
    chosen = lax.broadcasted_iota(jnp.int32, table.shape, 0) == slot_ref[0]
    chosen = jnp.sum(jnp.where(chosen, table, 0.0), axis=0, keepdims=True)
    all_lanes = lax.broadcasted_iota(jnp.int32, (1, 2 * B * B), 1)
    weight_ref[0:1] = jnp.broadcast_to(chosen[:, 0:1], (1, 2 * B * B))
    weight_ref[1:2] = jnp.where(all_lanes < B * B, -1.0, 1.0) * chosen[:, 1:2]
    per_owner = idx_ref.shape[2]
    most = 2 * per_owner // cells
    held_rows = most * B
    chunk = min(128, held_rows)
    earlier = (
        lax.broadcasted_iota(jnp.int32, (per_owner, per_owner), 0)
        < lax.broadcasted_iota(jnp.int32, (per_owner, per_owner), 1)
    ).astype(f32).astype(bf16)

    def ranks(o):
        cell_of = idx_ref[o, 0:1, :]
        marks = cell_of == lax.broadcasted_iota(jnp.int32, (cells, per_owner), 0).astype(f32)
        marks = jnp.where(marks, 1.0, 0.0)
        before = jnp.dot(marks.astype(bf16), earlier, preferred_element_type=f32)
        return cell_of, jnp.sum(marks * before, axis=0, keepdims=True)

    def index_owner(o, carry):
        cell_of, rank = ranks(o)
        place = jnp.where(cell_of == cell.astype(f32), rank, -1.0)

        def index_chunk(i, inner):
            slot = (lax.broadcasted_iota(jnp.int32, (chunk, per_owner), 0) + i * chunk) >> 3
            pick = jnp.where(place == slot.astype(f32), 1.0, 0.0)
            at = pl.ds(pl.multiple_of(i * chunk, chunk), chunk)
            for v in range(3):
                value = jnp.sum(pick * idx_ref[o, v + 1 : v + 2, :], axis=1, keepdims=True)
                slots[o, v, at] = jnp.broadcast_to(value, (chunk, 128))
            return inner

        lax.fori_loop(0, held_rows // chunk, index_chunk, 0)
        return carry

    lax.fori_loop(0, owners, index_owner, 0)
    apart = jnp.abs(r - c)
    for s in range(1, n):
        for h in range(HALVES):
            for side in range(2):
                k, there = from_side(side, s)

                @pl.when(there)
                def _():
                    l_copy(k, h, side, False).wait_recv()

                    @pl.when(can(side))
                    def _():
                        l_copy(k, h, side, False).start()

            for side in range(2):
                k, there = from_side(side, s)

                @pl.when(there)
                def _():
                    partial(k, h, False)

        if s >= 2:
            @pl.when(apart == s - 2)
            def _():
                finish()

    @pl.when(apart >= n - 2)
    def _():
        finish()

    lanes = 2 * B * B
    part_lanes = B * B

    def spread(total, transposed):
        at = lax.broadcasted_iota(jnp.int32, (2 * total, lanes), 0)
        to = lax.broadcasted_iota(jnp.int32, (2 * total, lanes), 1)
        half_of = (at >= total) == (to >= part_lanes)
        inner = ((to & (part_lanes - 1)) >> 3) if transposed else (to & 7)
        return jnp.where(half_of & ((at & 7) == inner), 1.0, 0.0).astype(bf16)

    spread_super = spread(size, False)
    spread_trail = spread(width, True)
    lane = lax.broadcasted_iota(jnp.int32, (chunk, lanes), 1)
    inside = lax.broadcasted_iota(jnp.int32, (chunk, lanes), 0) & 7
    keep_super = ((lane & (part_lanes - 1)) >> 3) == inside
    keep_trail = (lane & 7) == inside
    group = jnp.where(
        lax.broadcasted_iota(jnp.int32, (chunk // B, chunk), 0)
        == (lax.broadcasted_iota(jnp.int32, (chunk // B, chunk), 1) >> 3),
        1.0,
        0.0,
    ).astype(bf16)
    row_of = lax.broadcasted_iota(jnp.int32, (chunk, size), 1).astype(f32)
    row_in = (lax.broadcasted_iota(jnp.int32, (chunk, 1), 0) & 7).astype(f32)
    col_super = lax.broadcasted_iota(jnp.int32, (chunk, 2 * size), 1)
    col_super = jnp.where(col_super >= size, col_super - size, col_super).astype(f32)
    col_trail = lax.broadcasted_iota(jnp.int32, (chunk, 2 * width), 1)
    col_trail = jnp.where(col_trail >= width, col_trail - width, col_trail).astype(f32)
    last = float(B - 1)

    def trail_owner(o, carry):
        def trail_chunk(i, inner):
            at = pl.ds(pl.multiple_of(i * chunk, chunk), chunk)
            first_row = slots[o, 0, at][:, :1]
            first_trail = slots[o, 2, at][:, :1]
            pick = jnp.where(row_of == first_row + row_in, 1.0, 0.0).astype(bf16)
            taken = jnp.dot(pick, cz[c], preferred_element_type=f32)
            taken = jnp.where(
                (col_trail >= first_trail) & (col_trail <= first_trail + last), taken, 0.0
            ).astype(bf16)
            out_trail = jnp.dot(taken, spread_trail, preferred_element_type=f32)
            slots[o, 2, at] = jnp.where(keep_trail, out_trail, 0.0)
            return inner

        lax.fori_loop(0, held_rows // chunk, trail_chunk, 0)
        return carry

    for j in range(1, n):
        lx_wait(j)
    for t in range(1, n):
        for h in range(HALVES):
            for side in range(2):
                k, there = from_side(side, t)

                @pl.when(there)
                def _():
                    c_copy(k, h, side).wait_recv()

                    @pl.when(can(side))
                    def _():
                        c_copy(k, h, side).start()

            if h != min(1, HALVES - 1):
                continue
            if t == 1:
                accumulate(c, True)
                lax.fori_loop(0, owners, trail_owner, 0)
            else:
                for side in range(2):
                    k, there = from_side(side, t - 1)

                    @pl.when(there)
                    def _():
                        accumulate(k, False)

    for side in range(2):
        k, there = from_side(side, n - 1)

        @pl.when(there)
        def _():
            accumulate(k, False)

    def write(i, carry):
        at = pl.ds(pl.multiple_of(i * step, step), step)
        block_ref[at] = (inv_ref[at].astype(f32) - prod_ref[at]).astype(bf16)
        return carry

    lax.fori_loop(0, size // step, write, 0)

    def gather_owner(o, carry):
        def gather_chunk(i, inner):
            at = pl.ds(pl.multiple_of(i * chunk, chunk), chunk)
            first_row = slots[o, 0, at][:, :1]
            first_super = slots[o, 1, at][:, :1]
            pick = jnp.where(row_of == first_row + row_in, 1.0, 0.0).astype(bf16)
            taken = jnp.dot(pick, block_ref[...], preferred_element_type=f32)
            taken = jnp.where(
                (col_super >= first_super) & (col_super <= first_super + last), taken, 0.0
            ).astype(bf16)
            out_super = jnp.dot(taken, spread_super, preferred_element_type=f32)
            both = jnp.where(keep_super, out_super, 0.0) + slots[o, 2, at]
            value = jnp.dot(group, both.astype(bf16), preferred_element_type=f32)
            swapped = jnp.concatenate([value[:, part_lanes:], value[:, :part_lanes]], axis=1)
            to = pl.ds(pl.multiple_of(i * (chunk // B), chunk // B), chunk // B)
            term[o, to] = weight_ref[0:1] * value + weight_ref[1:2] * swapped
            return inner

        lax.fori_loop(0, held_rows // chunk, gather_chunk, 0)
        return carry

    def term_copy(j):
        to = lax.rem(me + j, owners)
        return pltpu.make_async_remote_copy(
            src_ref=term.at[to], dst_ref=pool.at[j], send_sem=term_send.at[j],
            recv_sem=term_recv.at[j], device_id={"pole": to}, device_id_type=MESH,
        )

    for j in range(1, owners):
        gather_owner(lax.rem(me + j, owners), 0)
        term_copy(j).start()
    gather_owner(me, 0)
    for j in range(1, owners):
        term_copy(j).wait_recv()
    total = term[me]
    for j in range(1, owners):
        total = total + pool[j]
    coll[cell] = total

    def coll_copy(j, at_col):
        at = r * n + at_col
        return pltpu.make_async_remote_copy(
            src_ref=coll.at[at], dst_ref=coll.at[at], send_sem=coll_send.at[j],
            recv_sem=coll_recv.at[at_col], device_id={"col": lax.rem(c + j, n)}, device_id_type=MESH,
        )

    def group_copy(j, at_row):
        at = pl.ds(at_row * n, n)
        return pltpu.make_async_remote_copy(
            src_ref=coll.at[at], dst_ref=coll.at[at], send_sem=coll_send.at[n + j],
            recv_sem=coll_recv.at[n + at_row], device_id={"row": lax.rem(r + j, n)}, device_id_type=MESH,
        )

    for j in range(1, n):
        coll_copy(j, c).start()
    cell_of, rank = ranks(me)
    target = jnp.broadcast_to(cell_of * most + rank, (128, per_owner))
    target = jnp.transpose(target)
    for j in range(1, n):
        coll_copy(j, lax.rem(c + j, n)).wait_recv()
    for j in range(1, n):
        group_copy(j, r).start()
    for j in range(1, n):
        group_copy(j, lax.rem(r + j, n)).wait_recv()
    for q in range(per_owner // 128):
        mine = target[q * 128 : (q + 1) * 128, :1]
        pick = jnp.where(
            mine == lax.broadcasted_iota(jnp.int32, (128, cells * most), 1).astype(f32), 1.0, 0.0
        ).astype(bf16)
        rest = coll[...].reshape(cells * most, lanes)
        summed = jnp.zeros((128, lanes), f32)
        for _ in range(3):
            top = rest.astype(bf16)
            rest = rest - top.astype(f32)
            summed = summed + jnp.dot(pick, top, preferred_element_type=f32)
        mine = proj_ref[q * 128 : (q + 1) * 128].astype(f32)
        dens_ref[q * 128 : (q + 1) * 128] = summed * jnp.concatenate([mine, mine], axis=1)

    for j in range(1, owners):
        term_copy(j).wait_send()
    for j in range(1, n):
        coll_copy(j, c).wait_send()
        group_copy(j, r).wait_send()
    for j in range(1, n):
        lx_copy(j).wait_send()
        for h in range(HALVES):
            rs_copy(lax.rem(r + j, n), h).wait_send()
    for s in range(n):
        for h in range(HALVES):
            for side in range(2):
                k, there = from_side(side, s)

                @pl.when(there & can(side))
                def _():
                    l_copy(k, h, side, s == 0).wait_send()
                    c_copy(k, h, side).wait_send()


def products(n, owners, lower, trail, inverse, pair_row, pair_col, table, slot, projector):
    size = lower.shape[0]
    wide = lower.shape[1]
    bf16 = jnp.bfloat16
    lanes = 2 * B * B
    per_owner = projector.shape[0]
    most = 2 * per_owner // (n * n)
    dma = pltpu.SemaphoreType.DMA
    vmem = pl.BlockSpec(memory_space=pltpu.VMEM)
    return pl.pallas_call(
        functools.partial(main_kernel, n),
        name="products",
        out_shape=(
            jax.ShapeDtypeStruct((size, 2 * size), bf16),
            jax.ShapeDtypeStruct((per_owner, lanes), jnp.float32),
        ),
        in_specs=[vmem] * 6 + [pl.BlockSpec(memory_space=pltpu.SMEM), vmem],
        out_specs=(vmem, vmem),
        scratch_shapes=[
            pltpu.VMEM((owners, 4, per_owner), jnp.float32),
            pltpu.VMEM((2, lanes), jnp.float32),
            pltpu.VMEM((owners, most, lanes), jnp.float32),
            pltpu.VMEM((owners, most, lanes), jnp.float32),
            pltpu.VMEM((n * n, most, lanes), jnp.float32),
            pltpu.VMEM((owners, 3, most * B, 128), jnp.float32),
            dma((owners,)),
            dma((owners,)),
            dma((2 * n,)),
            dma((2 * n,)),
            pltpu.VMEM((size, 2 * size), jnp.float32),
            pltpu.VMEM((n, size, wide), bf16),
            pltpu.VMEM((n, size, wide), bf16),
            pltpu.VMEM((n, size, wide), bf16),
            pltpu.VMEM((size, wide), jnp.float32),
            pltpu.VMEM((n, size, wide), bf16),
            pltpu.VMEM((n, size, wide), bf16),
            pltpu.VMEM((wide, wide), bf16),
            dma((2, n, HALVES)),
            dma((n, HALVES)),
            dma((n,)),
            dma((n,)),
            dma((n, HALVES)),
            dma((n, HALVES)),
            dma((2, n, HALVES)),
            dma((n, HALVES)),
        ],
        compiler_params=pltpu.CompilerParams(
            collective_id=0, has_side_effects=True, vmem_limit_bytes=40 * 1024 * 1024
        ),
    )(lower, trail, inverse, pair_row, pair_col, table, slot, projector)


def local(
    inverse_trail, lower_t, diag_inverse, pole_weight, pole_slot, pair_row, pair_col, projector
):
    trail = inverse_trail[0]
    lower = lower_t[0]
    inverse = diag_inverse[0]
    n = lax.axis_size("row")
    owners = lax.axis_size("pole")
    size = lower.shape[0]
    block, density = products(
        n,
        owners,
        lower.reshape(size, -1),
        trail.reshape(trail.shape[0], -1),
        inverse.reshape(size, -1),
        pair_row.reshape(owners, -1),
        pair_col.reshape(owners, -1),
        pole_weight,
        pole_slot,
        projector,
    )
    return block.reshape(1, size, 2, size), density


def solution(mesh):
    in_specs = (
        P("pole", "row", None, "col"),
        P("pole", "col", None, "row"),
        P("pole", "row", None, "col"),
        P(),
        P("pole"),
        P(),
        P(),
        P("pole", None),
    )
    out_specs = (P("pole", "row", None, "col"), P("pole", None))
    return jax.shard_map(local, mesh=mesh, in_specs=in_specs, out_specs=out_specs, check_vma=False)
```
